128 devices in a mesh: expert: 16 (over z, y), tensor: 8 (over x, core).
Axes of the slice: x: 4, y: 4, z: 4, core: 2. Of those that a mesh axis runs over, the one named last changes fastest.
Arguments:
- layer_input: bfloat16 [4096, 2, 4096], P('expert', None, 'tensor'), may hold values from -6 to 6
- base_input: bfloat16 [4096, 4096], P('expert', 'tensor'), may hold values from -6 to 6
- cotangent: bfloat16 [4096, 4096], P('expert', 'tensor'), may hold values from -6 to 6
- cross_weight: bfloat16 [16, 2, 4096, 4096], P('expert', None, 'tensor'), may hold values from -0.0625 to 0.0625
- cross_bias: float32 [16, 4096], P('expert', 'tensor'), may hold values from -3 to 3
- routes: int32 [4096, 2], P('expert'), may hold values from 0 to 15, as said below
- gate_values: float32 [4096, 2], P('expert'), may hold values from 0.2 to 1
Outputs:
- layer_out: bfloat16 [4096, 4096], P('expert', 'tensor')
- input_grad: bfloat16 [4096, 2, 4096], P('expert', None, 'tensor')
- base_grad: bfloat16 [4096, 4096], P('expert', 'tensor')
- weight_grad: bfloat16 [16, 2, 4096, 4096], P('expert', None, 'tensor')
- bias_grad: float32 [16, 4096], P('expert', 'tensor')
The draws below stay inside these ranges and needn't reach their ends.
Inputs may be any that keep to these rules, and one draw needn't show every extreme that they name: `routes`: each row names two different experts. Among the 256 rows of one index of expert (aligned blocks), no expert is named more than 48 times, and one expert, the same in every block, is named exactly 48 times in every block.
All inputs are finite; a program needn't handle non-finite values.
Results may differ from the reference program's by a relative error of at most 0.017.
Values may be sent and summed in bfloat16 or wider, within the bound.
A program may use at most 128 MiB of HBM per device.

```python
import jax
import jax.numpy as jnp
from jax import lax

D = 8192
OUT = 4096
EXPERTS = 16
ROW_DEV = 256
CAP = 48
ROWS = 4096
N_TENSOR = 8


def draw_routes(key, part):
    hot_key = jax.random.fold_in(key, 11)
    block_key = jax.random.fold_in(key, 12)
    hot_expert = jax.random.randint(hot_key, (), 0, EXPERTS, dtype=jnp.int32)
    spare = 2 * ROW_DEV - CAP

    def one_block(block_seed):
        pick_key = jax.random.fold_in(block_seed, 1)
        order_key = jax.random.fold_in(block_seed, 2)
        flip_key = jax.random.fold_in(block_seed, 3)
        chosen = jnp.sort(jax.random.permutation(pick_key, (EXPERTS - 1) * CAP)[:spare])
        others = (chosen // CAP).astype(jnp.int32)
        others = others + (others >= hot_expert).astype(jnp.int32)
        labels = jnp.concatenate([jnp.full((CAP,), hot_expert, jnp.int32), others])
        paired = jnp.stack([labels[:ROW_DEV], labels[ROW_DEV:]], axis=1)
        paired = paired[jax.random.permutation(order_key, ROW_DEV)]
        flips = jax.random.randint(flip_key, (ROW_DEV, 1), 0, 2, dtype=jnp.int32)
        return jnp.where(flips == 1, paired[:, ::-1], paired)
    seeds = jax.random.split(block_key, ROWS // ROW_DEV)
    return jax.vmap(one_block)(seeds).reshape(ROWS, 2).astype(jnp.int32)


def shard_levels(key, dims, cuts, least, top_value):
    level, own = 1.0, jax.random.fold_in(key, 6)
    for position, shards_of in cuts:
        heights = jnp.exp(jax.random.uniform(jax.random.fold_in(own, position), (shards_of,), jnp.float32, least / len(cuts), top_value / len(cuts)))
        level = level * jnp.repeat(heights, dims[position] // shards_of).reshape([-1 if axis == position else 1 for axis in range(len(dims))])
    return level


def scatter_about(own_key, extent, scale, most, cuts=(), kind=jnp.bfloat16):
    loudness = shard_levels(own_key, extent, cuts, -0.22, 0.18) if cuts else 1.0
    array = jax.random.normal(own_key, extent, jnp.float32) * scale * loudness
    return jnp.minimum(jnp.maximum(array, -most), most).astype(kind)


def setup_inputs(seed: int = 0) -> dict:
    arg_keys = jax.random.split(jax.random.key(seed), 8)
    return {
        "layer_input": scatter_about(arg_keys[0], (ROWS, 2, OUT), 1.0, 6.0, ((0, 16), (2, 8))),
        "base_input": scatter_about(arg_keys[1], (ROWS, OUT), 1.0, 6.0, ((0, 16), (1, 8))),
        "cotangent": scatter_about(arg_keys[2], (ROWS, OUT), 1.0, 6.0, ((0, 16), (1, 8))),
        "cross_weight": scatter_about(arg_keys[3], (EXPERTS, 2, OUT, OUT), D ** -0.5, 0.0625, ((0, 16), (2, 8))),
        "cross_bias": scatter_about(arg_keys[4], (EXPERTS, OUT), 0.5, 3.0, ((0, 16), (1, 8)), jnp.float32),
        "routes": draw_routes(jax.random.fold_in(arg_keys[7], 71), 0),
        "gate_values": jnp.clip(0.2 + 0.8 * jax.random.uniform(arg_keys[6], (ROWS, 2), jnp.float32) ** shard_levels(arg_keys[6], (ROWS, 2), ((0, 16),), -0.2, 0.2), 0.2, 1.0),
    }


def slot_positions(routes):
    blocks = ROWS // ROW_DEV
    flat_routes = routes.reshape(blocks, 2 * ROW_DEV)
    one_hot = (flat_routes[:, :, None] == jnp.arange(EXPERTS, dtype=jnp.int32)[None, None, :]).astype(jnp.int32)
    ranks = jnp.cumsum(one_hot, axis=1) - one_hot
    slots = lax.optimization_barrier(jnp.sum(ranks * one_hot, axis=2)).astype(jnp.int32)
    offsets = (jnp.arange(blocks, dtype=jnp.int32) * CAP)[:, None]
    return (offsets + slots).astype(jnp.int32).reshape(ROWS, 2)

def expert_pass(items):
    weight, bias, inputs, cots = items
    slots_all = inputs.shape[0]
    width = OUT // N_TENSOR
    split_inputs = inputs.astype(jnp.float32).reshape(slots_all, 2, N_TENSOR, width)
    split_weight = weight.astype(jnp.float32).reshape(2, N_TENSOR, width, OUT)
    parts = jnp.einsum('sptf,ptfo->tso', split_inputs, split_weight)
    parts = lax.optimization_barrier(parts.astype(jnp.bfloat16)).astype(jnp.float32)
    cross = (lax.optimization_barrier(jnp.sum(parts, axis=0)) + bias[None, :]).astype(jnp.bfloat16)
    scale = 1.0 / jnp.sqrt(jnp.float32(2 * ROW_DEV))
    cot_values = cots.astype(jnp.float32)
    weight_sum = jnp.einsum('spf,so->pfo', inputs.astype(jnp.float32), cot_values)
    weight_grad = (weight_sum * scale).astype(jnp.bfloat16)
    bias_grad = lax.optimization_barrier(jnp.sum(cot_values, axis=0)) * scale
    route_grads = jnp.einsum('so,pfo->spf', cot_values, weight.astype(jnp.float32)).astype(jnp.bfloat16)
    return (cross, weight_grad, bias_grad, route_grads)

def reference(layer_input, base_input, cotangent, cross_weight, cross_bias, routes, gate_values):
    positions = slot_positions(routes)
    slots_all = ROWS // ROW_DEV * CAP
    route_inputs = jnp.broadcast_to(layer_input[:, None, :, :], (ROWS, 2, 2, OUT))
    input_slots = jnp.zeros((EXPERTS, slots_all, 2, OUT), jnp.bfloat16).at[routes, positions].set(route_inputs)
    weighted = (cotangent.astype(jnp.float32) * base_input.astype(jnp.float32)).astype(jnp.bfloat16)
    route_cot = (gate_values[:, :, None] * weighted[:, None, :].astype(jnp.float32)).astype(jnp.bfloat16)
    cot_slots = jnp.zeros((EXPERTS, slots_all, OUT), jnp.bfloat16).at[routes, positions].set(route_cot)
    cross, weight_grad, bias_grad, route_grads = lax.map(expert_pass, (cross_weight, cross_bias, input_slots, cot_slots))
    cross_routes = cross[routes, positions].astype(jnp.float32)
    mixture = lax.optimization_barrier(jnp.sum(gate_values[:, :, None] * cross_routes, axis=1))
    gate_total = lax.optimization_barrier(jnp.sum(gate_values, axis=1))[:, None]
    layer_out = (base_input.astype(jnp.float32) * mixture + gate_total * layer_input[:, 0, :].astype(jnp.float32)).astype(jnp.bfloat16)
    picked = route_grads[routes, positions].astype(jnp.float32)
    grad_sum = lax.optimization_barrier(jnp.sum(picked, axis=1))
    grad_sum = grad_sum.at[:, 0, :].add(gate_total * cotangent.astype(jnp.float32))
    input_grad = grad_sum.astype(jnp.bfloat16)
    base_grad = (cotangent.astype(jnp.float32) * mixture).astype(jnp.bfloat16)
    return (layer_out, input_grad, base_grad, weight_grad, bias_grad)
```

```python
import functools

import jax
import jax.numpy as jnp
from jax import lax
from jax.experimental import pallas as pl
from jax.experimental.pallas import tpu as pltpu
from jax.sharding import PartitionSpec as P

MESH = pl.DeviceIdType.MESH
F32 = jnp.float32
BF16 = jnp.bfloat16
NN = (((1,), (0,)), ((), ()))
TN = (((0,), (0,)), ((), ()))
NT = (((1,), (1,)), ((), ()))


def dot(a, b, dims=NN):
    return lax.dot_general(a, b, dims, preferred_element_type=F32)


def kernel(
    sizes,
    x_ref, base_ref, cot_ref, w_ref, bias_ref, routes_ref, gates_ref,
    layer_out, input_grad, base_grad, weight_grad, bias_grad,
    pick, send_c, send_x, xa, xt, ca, wv, part_send, part_recv, own, far_send, far_recv,
    near_send, near_recv, cross_send, cross_back, grad_acc, grad_send, grad_back, wg,
    w_sem, wg_sem, c_ss, c_rs, x_ss, x_rs, ag_ss, ag_rs, p_ss, p_rs, far_ss, far_rs,
    near_ss, near_rs, g_ss, g_rs, y_ss, y_rs,
):
    experts, rows, width, cap = sizes
    slots = experts * cap
    feats = 2 * width
    half = experts // 2
    me = lax.axis_index("expert")
    tensor = lax.axis_index("tensor")
    chip, core = tensor // 2, lax.rem(tensor, 2)
    other = 1 - core

    def at(step, which):
        return lax.rem(chip + step, 4) * 2 + which

    own_t, left_t, right_t, far_t = at(0, core), at(3, core), at(1, core), at(2, core)
    partner = at(0, other)

    def peer(d):
        return lax.rem(me + d, experts)

    barrier = pltpu.get_barrier_semaphore()

    def greet(d, carry):
        pl.semaphore_signal(barrier, inc=1, device_id={"expert": peer(d)}, device_id_type=MESH)
        return carry

    lax.fori_loop(1, experts, greet, 0)
    for t in (partner, left_t, right_t):
        pl.semaphore_signal(barrier, inc=1, device_id={"tensor": t}, device_id_type=MESH)

    def w_copy(t):
        return pltpu.make_async_copy(
            w_ref.at[:, pl.ds(pl.multiple_of(t * width, width), width)], wv.at[t], w_sem.at[t]
        )

    def start_w(t, carry):
        w_copy(t).start()
        return carry

    lax.fori_loop(0, 8, start_w, 0)

    below = (
        lax.broadcasted_iota(jnp.int32, (rows, rows), 1)
        < lax.broadcasted_iota(jnp.int32, (rows, rows), 0)
    ).astype(F32).astype(BF16)
    expert_id = lax.broadcasted_iota(jnp.int32, (rows, experts), 1)
    first = expert_id.astype(F32) * float(cap)
    slot_id = lax.broadcasted_iota(jnp.int32, (rows, slots), 1).astype(F32)
    routes = routes_ref[...]
    gates = gates_ref[...]
    weighted = (cot_ref[...].astype(F32) * base_ref[...].astype(F32)).astype(BF16).astype(F32)
    sent = None
    for k in range(2):
        named = (routes[:, k : k + 1] == expert_id).astype(F32)
        place = first + dot(below, named.astype(BF16))
        if k == 0:
            first = first + jnp.sum(named, axis=0, keepdims=True)
        position = jnp.sum(named * place, axis=1, keepdims=True)
        chosen = (slot_id == position).astype(F32).astype(BF16)
        pick[k] = chosen
        route_cot = (gates[:, k : k + 1] * weighted).astype(BF16)
        piece = dot(chosen, route_cot, TN)
        sent = piece if sent is None else sent + piece
    send_c[...] = sent.astype(BF16).reshape(experts, cap, width)

    def over(src, dst, ss, rs, d):
        return pltpu.make_async_remote_copy(
            src_ref=src.at[peer(d)], dst_ref=dst.at[me], send_sem=ss.at[d], recv_sem=rs.at[me],
            device_id={"expert": peer(d)}, device_id_type=MESH,
        )

    def exchange(src, dst, ss, rs):
        def body(d, carry):
            over(src, dst, ss, rs, d).start()
            return carry

        lax.fori_loop(1, experts, body, 0)

    def landed(dst, ss, rs):
        def body(d, carry):
            source = peer(d)
            pltpu.make_async_remote_copy(
                src_ref=dst.at[source], dst_ref=dst.at[source], send_sem=ss.at[d],
                recv_sem=rs.at[source], device_id={"expert": source}, device_id_type=MESH,
            ).wait_recv()
            return carry

        lax.fori_loop(1, experts, body, 0)

    def drain(src, dst, ss, rs):
        def body(d, carry):
            over(src, dst, ss, rs, d).wait_send()
            return carry

        lax.fori_loop(1, experts, body, 0)

    pl.semaphore_wait(barrier, experts + 2)
    ca_own = ca.at[own_t]
    exchange(send_c, ca_own, c_ss, c_rs)
    send_x[...] = dot(pick[0] + pick[1], x_ref[...], TN).astype(BF16).reshape(experts, cap, feats)
    exchange(send_x, xa, x_ss, x_rs)
    ca[own_t, me] = send_c[me]
    xa[me] = send_x[me]

    def wait_w(t, carry):
        w_copy(t).wait()
        return carry

    lax.fori_loop(0, 8, wait_w, 0)

    low, high, whole = pl.ds(0, half), pl.ds(half, half), pl.ds(0, experts)
    moves = [
        (own_t, low, right_t, left_t),
        (own_t, high, right_t, left_t),
        (own_t, high, left_t, right_t),
        (own_t, low, left_t, right_t),
        (own_t, whole, partner, partner),
        (left_t, low, right_t, far_t),
        (right_t, high, left_t, far_t),
        (left_t, whole, partner, at(3, other)),
        (right_t, whole, partner, at(1, other)),
        (far_t, whole, partner, at(2, other)),
    ]

    def move(i):
        block, part, target, _ = moves[i]
        region = ca.at[block, part]
        return pltpu.make_async_remote_copy(
            src_ref=region, dst_ref=region, send_sem=ag_ss.at[i], recv_sem=ag_rs.at[i],
            device_id={"tensor": target}, device_id_type=MESH,
        )

    def arrived(i):
        _, part, _, block = moves[i]
        region = ca.at[block, part]
        pltpu.make_async_remote_copy(
            src_ref=region, dst_ref=region, send_sem=ag_ss.at[i], recv_sem=ag_rs.at[i],
            device_id={"tensor": partner}, device_id_type=MESH,
        ).wait_recv()

    landed(ca_own, c_ss, c_rs)
    for i in (0, 2, 1, 3, 4):
        move(i).start()

    def cot_block(t):
        return ca[t].reshape(slots, width)

    def grads_of(t):
        return dot(cot_block(t), wv[t], NT)

    scale = 1.0 / (2.0 * rows) ** 0.5
    bias_grad[...] = jnp.sum(cot_block(own_t).astype(F32), axis=0, keepdims=True) * scale
    grad_acc[...] = grads_of(own_t)
    arrived(4)
    grad_acc[...] += grads_of(partner)
    arrived(0)
    move(5).start()
    arrived(2)
    move(6).start()
    arrived(1)
    move(7).start()
    arrived(3)
    move(8).start()
    landed(xa, x_ss, x_rs)

    def partial(t):
        return dot(xa[...].reshape(slots, feats), wv[t])

    def pair(k):
        return pltpu.make_async_remote_copy(
            src_ref=part_send.at[k], dst_ref=part_recv.at[k], send_sem=p_ss.at[k],
            recv_sem=p_rs.at[k], device_id={"tensor": partner}, device_id_type=MESH,
        )

    def to_partner(i, carry):
        k = lax.rem(i + 2, 4)
        part_send[k] = partial(at(k, other)).astype(BF16)
        pair(k).start()
        return carry

    lax.fori_loop(0, 4, to_partner, 0)

    middle = slots // 2

    def far(i):
        target = (right_t, left_t)[i]
        return pltpu.make_async_remote_copy(
            src_ref=far_send.at[i], dst_ref=far_recv.at[i], send_sem=far_ss.at[i],
            recv_sem=far_rs.at[i], device_id={"tensor": target}, device_id_type=MESH,
        )

    def near(i):
        target = (right_t, left_t)[i]
        return pltpu.make_async_remote_copy(
            src_ref=near_send.at[i], dst_ref=near_recv.at[i], send_sem=near_ss.at[i],
            recv_sem=near_rs.at[i], device_id={"tensor": target}, device_id_type=MESH,
        )

    mine = partial(at(2, core))
    pair(2).wait_recv()
    far_send[...] = (mine + part_recv[2].astype(F32)).astype(BF16).reshape(2, middle, width)
    far(0).start()
    far(1).start()

    def chip_sum(i, carry):
        k = lax.rem(2 * i + 1, 5)
        own[i] = partial(at(k, core))
        pair(k).wait_recv()
        own[i] += part_recv[k].astype(F32)
        return carry

    lax.fori_loop(0, 3, chip_sum, 0)

    def add_grads(t):
        grad_acc[...] += grads_of(t)

    add_grads(left_t)
    add_grads(right_t)
    arrived(5)
    arrived(6)
    move(9).start()
    arrived(7)
    add_grads(at(3, other))
    arrived(8)
    add_grads(at(1, other))
    add_grads(far_t)
    arrived(9)
    grad_send[...] = (
        (grad_acc[...] + grads_of(at(2, other))).astype(BF16).reshape(experts, cap, feats)
    )
    exchange(grad_send, grad_back, g_ss, g_rs)
    grad_back[me] = grad_send[me]

    for i in range(2):
        far(i).wait_recv()
        rest = pl.ds(i * middle, middle)
        keep = pl.ds((1 - i) * middle, middle)
        near_send[i, rest] = (own[i, rest] + far_recv[i].astype(F32)).astype(BF16)
        near_send[i, keep] = own[i, keep].astype(BF16)
        near(i).start()

    xt[...] = xa[...].reshape(slots, feats).T

    def wg_copy(t, slot):
        return pltpu.make_async_copy(
            wg.at[slot],
            weight_grad.at[:, pl.ds(pl.multiple_of(t * width, width), width)],
            wg_sem.at[slot],
        )

    def weight_block(t, carry):
        slot = lax.rem(t, 2)

        @pl.when(t >= 2)
        def _():
            wg_copy(t - 2, slot).wait()

        wg[slot] = (dot(xt[...], cot_block(t)) * scale).astype(BF16)
        wg_copy(t, slot).start()
        return carry

    lax.fori_loop(0, 8, weight_block, 0)

    near(0).wait_recv()
    near(1).wait_recv()
    cross = own[2] + near_recv[0].astype(F32) + near_recv[1].astype(F32) + bias_ref[...]
    cross_send[...] = cross.astype(BF16).reshape(experts, cap, width)
    exchange(cross_send, cross_back, y_ss, y_rs)
    cross_back[me] = cross_send[me]

    gate0, gate1 = gates_ref[:, 0:1], gates_ref[:, 1:2]
    gate_total = gate0 + gate1
    cot = cot_ref[...].astype(F32)
    landed(grad_back, g_ss, g_rs)
    grad_sum = dot(pick[0] + pick[1], grad_back[...].reshape(slots, feats))
    input_grad[:, :width] = (grad_sum[:, :width] + gate_total * cot).astype(BF16)
    input_grad[:, width:] = grad_sum[:, width:].astype(BF16)

    landed(cross_back, y_ss, y_rs)
    back = cross_back[...].reshape(slots, width)
    mixture = gate0 * dot(pick[0], back) + gate1 * dot(pick[1], back)
    layer_out[...] = (
        base_ref[...].astype(F32) * mixture + gate_total * x_ref[:, :width].astype(F32)
    ).astype(BF16)
    base_grad[...] = (cot * mixture).astype(BF16)

    wg_copy(6, 0).wait()
    wg_copy(7, 1).wait()
    drain(send_c, ca_own, c_ss, c_rs)
    drain(send_x, xa, x_ss, x_rs)
    for i in range(10):
        move(i).wait_send()
    for k in range(4):
        pair(k).wait_send()
    for i in range(2):
        far(i).wait_send()
        near(i).wait_send()
    drain(grad_send, grad_back, g_ss, g_rs)
    drain(cross_send, cross_back, y_ss, y_rs)


def per_device(layer_input, base_input, cotangent, cross_weight, cross_bias, routes, gate_values):
    rows, _, width = layer_input.shape
    full_out = cross_weight.shape[3]
    experts = lax.axis_size("expert")
    cap = (3 * rows + experts - 1) // experts
    slots, feats = experts * cap, 2 * width
    vmem = pl.BlockSpec(memory_space=pltpu.VMEM)
    hbm = pl.BlockSpec(memory_space=pl.ANY)
    dma = pltpu.SemaphoreType.DMA
    layer_out, input_grad, base_grad, weight_grad, bias_grad = pl.pallas_call(
        functools.partial(kernel, (experts, rows, width, cap)),
        out_shape=(
            jax.ShapeDtypeStruct((rows, width), BF16),
            jax.ShapeDtypeStruct((rows, feats), BF16),
            jax.ShapeDtypeStruct((rows, width), BF16),
            jax.ShapeDtypeStruct((feats, full_out), BF16),
            jax.ShapeDtypeStruct((1, width), F32),
        ),
        in_specs=[vmem, vmem, vmem, hbm, vmem, vmem, vmem],
        out_specs=(vmem, vmem, vmem, hbm, vmem),
        scratch_shapes=[
            pltpu.VMEM((2, rows, slots), BF16),
            pltpu.VMEM((experts, cap, width), BF16),
            pltpu.VMEM((experts, cap, feats), BF16),
            pltpu.VMEM((experts, cap, feats), BF16),
            pltpu.VMEM((feats, slots), BF16),
            pltpu.VMEM((8, experts, cap, width), BF16),
            pltpu.VMEM((8, feats, width), BF16),
            pltpu.VMEM((4, slots, width), BF16),
            pltpu.VMEM((4, slots, width), BF16),
            pltpu.VMEM((3, slots, width), F32),
            pltpu.VMEM((2, slots // 2, width), BF16),
            pltpu.VMEM((2, slots // 2, width), BF16),
            pltpu.VMEM((2, slots, width), BF16),
            pltpu.VMEM((2, slots, width), BF16),
            pltpu.VMEM((experts, cap, width), BF16),
            pltpu.VMEM((experts, cap, width), BF16),
            pltpu.VMEM((slots, feats), F32),
            pltpu.VMEM((experts, cap, feats), BF16),
            pltpu.VMEM((experts, cap, feats), BF16),
            pltpu.VMEM((2, feats, width), BF16),
            dma((8,)), dma((2,)),
            dma((experts,)), dma((experts,)), dma((experts,)), dma((experts,)),
            dma((10,)), dma((10,)), dma((4,)), dma((4,)), dma((2,)), dma((2,)),
            dma((2,)), dma((2,)),
            dma((experts,)), dma((experts,)), dma((experts,)), dma((experts,)),
        ],
        compiler_params=pltpu.CompilerParams(
            collective_id=0, has_side_effects=True, vmem_limit_bytes=62 * 1024 * 1024
        ),
        name="cross_experts",
    )(
        layer_input.reshape(rows, feats), base_input, cotangent,
        cross_weight.reshape(feats, full_out), cross_bias, routes, gate_values,
    )
    return (
        layer_out,
        input_grad.reshape(rows, 2, width),
        base_grad,
        weight_grad.reshape(1, 2, width, full_out),
        bias_grad,
    )


def solution(mesh):
    in_specs = (
        P("expert", None, "tensor"),
        P("expert", "tensor"),
        P("expert", "tensor"),
        P("expert", None, "tensor", None),
        P("expert", "tensor"),
        P("expert", None),
        P("expert", None),
    )
    out_specs = (
        P("expert", "tensor"),
        P("expert", None, "tensor"),
        P("expert", "tensor"),
        P("expert", None, "tensor", None),
        P("expert", "tensor"),
    )
    return jax.shard_map(
        per_device, mesh=mesh, in_specs=in_specs, out_specs=out_specs, check_vma=False
    )
```

```python
import functools

import jax
import jax.numpy as jnp
from jax import lax
from jax.experimental import pallas as pl
from jax.experimental.pallas import tpu as pltpu
from jax.sharding import PartitionSpec as P

MESH = pl.DeviceIdType.MESH
F32 = jnp.float32
BF16 = jnp.bfloat16
CHUNKS = 3
NN = (((1,), (0,)), ((), ()))
TN = (((0,), (0,)), ((), ()))
NT = (((1,), (1,)), ((), ()))


def dot(a, b, dims=NN):
    return lax.dot_general(a, b, dims, preferred_element_type=F32)


def kernel(
    sizes,
    x_ref, base_ref, cot_ref, w_ref, bias_ref, routes_ref, gates_ref,
    layer_out, input_grad, base_grad, weight_grad, bias_grad,
    pick, gate_cols, send_c, send_x, xa, xt, ca, wv, part_send, part_recv, own,
    far_send, far_recv, near_send, near_recv, cross_send, cross_back,
    grad_acc, grad_send, grad_back, wg,
    w_sem, wg_sem, c_ss, c_rs, x_ss, x_rs, ag_ss, ag_rs, p_ss, p_rs, far_ss, far_rs,
    near_ss, near_rs, g_ss, g_rs, y_ss, y_rs,
):
    experts, rows, width, lot = sizes
    lot_slots = experts * lot
    slots = CHUNKS * lot_slots
    feats = 2 * width
    half = experts // 2
    middle = half * lot
    me = lax.axis_index("expert")
    tensor = lax.axis_index("tensor")
    chip, core = tensor // 2, lax.rem(tensor, 2)
    other = 1 - core

    def at(step, which):
        return lax.rem(chip + step, 4) * 2 + which

    own_t, left_t, right_t, far_t = at(0, core), at(3, core), at(1, core), at(2, core)
    partner = at(0, other)

    def peer(d):
        return lax.rem(me + d, experts)

    def loop(start, stop, step):
        def run(i, carry):
            step(i)
            return carry

        lax.fori_loop(start, stop, run, 0)

    barrier = pltpu.get_barrier_semaphore()

    def greet(d):
        pl.semaphore_signal(barrier, inc=1, device_id={"expert": peer(d)}, device_id_type=MESH)

    loop(1, experts, greet)
    for t in (partner, left_t, right_t):
        pl.semaphore_signal(barrier, inc=1, device_id={"tensor": t}, device_id_type=MESH)

    def w_copy(t):
        return pltpu.make_async_copy(
            w_ref.at[:, pl.ds(pl.multiple_of(t * width, width), width)], wv.at[t], w_sem.at[t]
        )

    loop(0, 8, lambda t: w_copy(t).start())

    below = (
        lax.broadcasted_iota(jnp.int32, (rows, rows), 1)
        < lax.broadcasted_iota(jnp.int32, (rows, rows), 0)
    ).astype(F32).astype(BF16)
    expert_id = lax.broadcasted_iota(jnp.int32, (rows, experts), 1).astype(F32)
    slot_id = lax.broadcasted_iota(jnp.int32, (rows, slots), 1).astype(F32)
    columns = jnp.concatenate(
        [routes_ref[...].astype(F32), gates_ref[...], jnp.zeros((4, rows), F32)], axis=0
    ).T
    gate_cols[...] = columns
    weighted = (cot_ref[...].astype(F32) * base_ref[...].astype(F32)).astype(BF16).astype(F32)
    sent, before = None, 0.0
    for k in range(2):
        named = (columns[:, k : k + 1] == expert_id).astype(F32)
        place = jnp.sum(
            named * (before + dot(below, named.astype(BF16))), axis=1, keepdims=True
        )
        if k == 0:
            before = jnp.sum(named, axis=0, keepdims=True)
        position = place + float(lot) * jnp.sum(named * expert_id, axis=1, keepdims=True)
        for q in range(1, CHUNKS):
            position += float(lot_slots - lot) * (place >= float(q * lot)).astype(F32)
        chosen = (slot_id == position).astype(F32).astype(BF16)
        pick[k] = chosen
        route_cot = (columns[:, k + 2 : k + 3] * weighted).astype(BF16)
        piece = dot(chosen, route_cot, TN)
        sent = piece if sent is None else sent + piece
    send_c[...] = sent.astype(BF16).reshape(CHUNKS, experts, lot, width)

    def over(src, dst, ss, rs, q, d):
        return pltpu.make_async_remote_copy(
            src_ref=src.at[q, peer(d)], dst_ref=dst.at[q, me], send_sem=ss.at[q, d],
            recv_sem=rs.at[q, me], device_id={"expert": peer(d)}, device_id_type=MESH,
        )

    def exchange(src, dst, ss, rs, q):
        loop(1, experts, lambda d: over(src, dst, ss, rs, q, d).start())

    def landed(dst, ss, rs, q):
        def take(d):
            source = peer(d)
            pltpu.make_async_remote_copy(
                src_ref=dst.at[q, source], dst_ref=dst.at[q, source], send_sem=ss.at[q, d],
                recv_sem=rs.at[q, source], device_id={"expert": source}, device_id_type=MESH,
            ).wait_recv()

        loop(1, experts, take)

    def drain(src, dst, ss, rs):
        for q in range(CHUNKS):
            loop(1, experts, lambda d, q=q: over(src, dst, ss, rs, q, d).wait_send())

    pl.semaphore_wait(barrier, experts + 2)
    ca_own = ca.at[own_t]
    for q in range(CHUNKS):
        exchange(send_c, ca_own, c_ss, c_rs, q)
    send_x[...] = (
        dot(pick[0] + pick[1], x_ref[...], TN).astype(BF16).reshape(CHUNKS, experts, lot, feats)
    )
    for q in range(CHUNKS):
        exchange(send_x, xa, x_ss, x_rs, q)
        ca[own_t, q, me] = send_c[q, me]
        xa[q, me] = send_x[q, me]

    low, high, whole = pl.ds(0, half), pl.ds(half, half), pl.ds(0, experts)
    moves = [
        (own_t, low, right_t, left_t),
        (own_t, high, right_t, left_t),
        (own_t, high, left_t, right_t),
        (own_t, low, left_t, right_t),
        (own_t, whole, partner, partner),
        (left_t, low, right_t, far_t),
        (right_t, high, left_t, far_t),
        (left_t, whole, partner, at(3, other)),
        (right_t, whole, partner, at(1, other)),
        (far_t, whole, partner, at(2, other)),
    ]

    def move(i, q):
        block, part, target, _ = moves[i]
        region = ca.at[block, q, part]
        return pltpu.make_async_remote_copy(
            src_ref=region, dst_ref=region, send_sem=ag_ss.at[i, q], recv_sem=ag_rs.at[i, q],
            device_id={"tensor": target}, device_id_type=MESH,
        )

    def arrived(i, q):
        _, part, _, block = moves[i]
        region = ca.at[block, q, part]
        pltpu.make_async_remote_copy(
            src_ref=region, dst_ref=region, send_sem=ag_ss.at[i, q], recv_sem=ag_rs.at[i, q],
            device_id={"tensor": partner}, device_id_type=MESH,
        ).wait_recv()

    def arrived_all(i):
        for q in range(CHUNKS):
            arrived(i, q)

    for q in range(CHUNKS):
        landed(ca_own, c_ss, c_rs, q)
        for i in (0, 2, 1, 3, 4):
            move(i, q).start()

    def cot_block(t):
        return ca[t].reshape(slots, width)

    def grads_of(t):
        return dot(cot_block(t), wv[t], NT)

    def add_grads(t):
        grad_acc[...] += grads_of(t)

    def pass_on(q):
        arrived(0, q)
        move(5, q).start()
        arrived(2, q)
        move(6, q).start()
        arrived(1, q)
        move(7, q).start()
        arrived(3, q)
        move(8, q).start()

    def partial(t, q):
        return dot(xa[q].reshape(lot_slots, feats), wv[t])

    def pair(k, q):
        return pltpu.make_async_remote_copy(
            src_ref=part_send.at[k, q], dst_ref=part_recv.at[k, q], send_sem=p_ss.at[k, q],
            recv_sem=p_rs.at[k, q], device_id={"tensor": partner}, device_id_type=MESH,
        )

    def ring(send, recv, ss, rs, i, q):
        return pltpu.make_async_remote_copy(
            src_ref=send.at[i, q], dst_ref=recv.at[i, q], send_sem=ss.at[i, q],
            recv_sem=rs.at[i, q], device_id={"tensor": (right_t, left_t)[i]},
            device_id_type=MESH,
        )

    def far(i, q):
        return ring(far_send, far_recv, far_ss, far_rs, i, q)

    def near(i, q):
        return ring(near_send, near_recv, near_ss, near_rs, i, q)

    def to_partner(k, q):
        part_send[k, q] = partial(at(k, other), q).astype(BF16)
        pair(k, q).start()

    def to_far(q):
        mine = partial(far_t, q)
        pair(2, q).wait_recv()
        total = (mine + part_recv[2, q].astype(F32)).astype(BF16)
        far_send[0, q] = total[:middle]
        far_send[1, q] = total[middle:]
        far(0, q).start()
        far(1, q).start()

    def chip_sum(i, k, q):
        mine = partial(at(k, core), q)
        pair(k, q).wait_recv()
        own[i, q] = mine + part_recv[k, q].astype(F32)

    def to_near(q):
        for i in range(2):
            far(i, q).wait_recv()
            rest, keep = pl.ds(i * middle, middle), pl.ds((1 - i) * middle, middle)
            near_send[i, q, rest] = (own[i, q, rest] + far_recv[i, q].astype(F32)).astype(BF16)
            near_send[i, q, keep] = own[i, q, keep].astype(BF16)
            near(i, q).start()

    def to_rows(q):
        near(0, q).wait_recv()
        near(1, q).wait_recv()
        cross = own[2, q] + near_recv[0, q].astype(F32) + near_recv[1, q].astype(F32)
        cross = (cross + bias_ref[...]).astype(BF16)
        cross_send[q] = cross.reshape(experts, lot, width)
        exchange(cross_send, cross_back, y_ss, y_rs, q)
        cross_back[q, me] = cross_send[q, me]

    scale = 1.0 / (2.0 * rows) ** 0.5
    bias_grad[...] = jnp.sum(cot_block(own_t).astype(F32), axis=0, keepdims=True) * scale
    loop(0, 8, lambda t: w_copy(t).wait())
    grad_acc[...] = grads_of(own_t)
    pass_on(0)
    arrived_all(4)
    add_grads(partner)
    pass_on(1)
    landed(xa, x_ss, x_rs, 0)
    to_partner(2, 0)
    pass_on(2)
    landed(xa, x_ss, x_rs, 1)
    to_partner(2, 1)
    to_far(0)
    add_grads(left_t)
    add_grads(right_t)
    landed(xa, x_ss, x_rs, 2)
    to_partner(2, 2)
    to_far(1)
    to_far(2)
    arrived_all(7)
    add_grads(at(3, other))
    arrived_all(8)
    add_grads(at(1, other))
    for q in range(CHUNKS):
        arrived(5, q)
        arrived(6, q)
        move(9, q).start()
    add_grads(far_t)
    loop(0, 2 * CHUNKS, lambda n: to_partner(1 + 2 * lax.rem(n, 2), n // 2))
    arrived_all(9)
    grad_send[...] = (
        (grad_acc[...] + grads_of(at(2, other)))
        .astype(BF16)
        .reshape(CHUNKS, experts, lot, feats)
    )
    for q in range(CHUNKS):
        exchange(grad_send, grad_back, g_ss, g_rs, q)
        grad_back[q, me] = grad_send[q, me]
    loop(0, 2 * CHUNKS, lambda n: chip_sum(lax.rem(n, 2), 1 + 2 * lax.rem(n, 2), n // 2))
    loop(0, CHUNKS, to_near)
    loop(0, CHUNKS, lambda q: to_partner(0, q))
    loop(0, CHUNKS, lambda q: chip_sum(2, 0, q))

    xt[...] = xa[...].reshape(slots, feats).T

    def wg_copy(t, slot):
        return pltpu.make_async_copy(
            wg.at[slot],
            weight_grad.at[:, pl.ds(pl.multiple_of(t * width, width), width)],
            wg_sem.at[slot],
        )

    def weight_block(t):
        slot = lax.rem(t, 2)

        @pl.when(t >= 2)
        def _():
            wg_copy(t - 2, slot).wait()

        wg[slot] = (dot(xt[...], cot_block(t)) * scale).astype(BF16)
        wg_copy(t, slot).start()

    loop(0, 4, weight_block)
    to_rows(0)
    loop(4, 6, weight_block)
    to_rows(1)
    loop(6, 8, weight_block)
    to_rows(2)

    gate0, gate1 = gate_cols[:, 2:3], gate_cols[:, 3:4]
    gate_total = gate0 + gate1
    cot = cot_ref[...].astype(F32)
    for q in range(CHUNKS):
        landed(grad_back, g_ss, g_rs, q)
    grad_sum = dot(pick[0] + pick[1], grad_back[...].reshape(slots, feats))
    input_grad[:, :width] = (grad_sum[:, :width] + gate_total * cot).astype(BF16)
    input_grad[:, width:] = grad_sum[:, width:].astype(BF16)

    for q in range(CHUNKS):
        landed(cross_back, y_ss, y_rs, q)
    back = cross_back[...].reshape(slots, width)
    mixture = gate0 * dot(pick[0], back) + gate1 * dot(pick[1], back)
    layer_out[...] = (
        base_ref[...].astype(F32) * mixture + gate_total * x_ref[:, :width].astype(F32)
    ).astype(BF16)
    base_grad[...] = (cot * mixture).astype(BF16)

    wg_copy(6, 0).wait()
    wg_copy(7, 1).wait()
    drain(send_c, ca_own, c_ss, c_rs)
    drain(send_x, xa, x_ss, x_rs)
    for q in range(CHUNKS):
        for i in range(10):
            move(i, q).wait_send()
        for k in range(4):
            pair(k, q).wait_send()
        for i in range(2):
            far(i, q).wait_send()
            near(i, q).wait_send()
    drain(grad_send, grad_back, g_ss, g_rs)
    drain(cross_send, cross_back, y_ss, y_rs)


def per_device(layer_input, base_input, cotangent, cross_weight, cross_bias, routes, gate_values):
    rows, _, width = layer_input.shape
    full_out = cross_weight.shape[3]
    experts = lax.axis_size("expert")
    cap = (3 * rows + experts - 1) // experts
    lot = cap // CHUNKS
    slots, feats = experts * cap, 2 * width
    vmem = pl.BlockSpec(memory_space=pltpu.VMEM)
    hbm = pl.BlockSpec(memory_space=pl.ANY)
    dma = pltpu.SemaphoreType.DMA

    def routed(features):
        return [pltpu.VMEM((CHUNKS, experts, lot, features), BF16)]

    def pairs(*shape):
        return [dma(shape), dma(shape)]

    layer_out, input_grad, base_grad, weight_grad, bias_grad = pl.pallas_call(
        functools.partial(kernel, (experts, rows, width, lot)),
        out_shape=(
            jax.ShapeDtypeStruct((rows, width), BF16),
            jax.ShapeDtypeStruct((rows, feats), BF16),
            jax.ShapeDtypeStruct((rows, width), BF16),
            jax.ShapeDtypeStruct((feats, full_out), BF16),
            jax.ShapeDtypeStruct((1, width), F32),
        ),
        in_specs=[vmem, vmem, vmem, hbm, vmem, vmem, vmem],
        out_specs=(vmem, vmem, vmem, hbm, vmem),
        scratch_shapes=[
            pltpu.VMEM((2, rows, slots), BF16),
            pltpu.VMEM((rows, 8), F32),
            *routed(width), *routed(feats), *routed(feats),
            pltpu.VMEM((feats, slots), BF16),
            pltpu.VMEM((8, CHUNKS, experts, lot, width), BF16),
            pltpu.VMEM((8, feats, width), BF16),
            pltpu.VMEM((4, CHUNKS, experts * lot, width), BF16),
            pltpu.VMEM((4, CHUNKS, experts * lot, width), BF16),
            pltpu.VMEM((3, CHUNKS, experts * lot, width), F32),
            pltpu.VMEM((2, CHUNKS, experts // 2 * lot, width), BF16),
            pltpu.VMEM((2, CHUNKS, experts // 2 * lot, width), BF16),
            pltpu.VMEM((2, CHUNKS, experts * lot, width), BF16),
            pltpu.VMEM((2, CHUNKS, experts * lot, width), BF16),
            *routed(width), *routed(width),
            pltpu.VMEM((slots, feats), F32),
            *routed(feats), *routed(feats),
            pltpu.VMEM((2, feats, width), BF16),
            dma((8,)), dma((2,)),
            *pairs(CHUNKS, experts), *pairs(CHUNKS, experts),
            *pairs(10, CHUNKS), *pairs(4, CHUNKS), *pairs(2, CHUNKS), *pairs(2, CHUNKS),
            *pairs(CHUNKS, experts), *pairs(CHUNKS, experts),
        ],
        compiler_params=pltpu.CompilerParams(
            collective_id=0, has_side_effects=True, vmem_limit_bytes=62 * 1024 * 1024
        ),
        name="cross_experts",
    )(
        layer_input.reshape(rows, feats), base_input, cotangent,
        cross_weight.reshape(feats, full_out), cross_bias, routes.T, gate_values.T,
    )
    return (
        layer_out,
        input_grad.reshape(rows, 2, width),
        base_grad,
        weight_grad.reshape(1, 2, width, full_out),
        bias_grad,
    )


def solution(mesh):
    in_specs = (
        P("expert", None, "tensor"),
        P("expert", "tensor"),
        P("expert", "tensor"),
        P("expert", None, "tensor", None),
        P("expert", "tensor"),
        P("expert", None),
        P("expert", None),
    )
    out_specs = (
        P("expert", "tensor"),
        P("expert", None, "tensor"),
        P("expert", "tensor"),
        P("expert", None, "tensor", None),
        P("expert", "tensor"),
    )
    return jax.shard_map(
        per_device, mesh=mesh, in_specs=in_specs, out_specs=out_specs, check_vma=False
    )
```

```python
import functools

import jax
import jax.numpy as jnp
from jax import lax
from jax.experimental import pallas as pl
from jax.experimental.pallas import tpu as pltpu
from jax.sharding import PartitionSpec as P

MESH = pl.DeviceIdType.MESH
F32 = jnp.float32
BF16 = jnp.bfloat16
CHUNKS = 3
NN = (((1,), (0,)), ((), ()))
TN = (((0,), (0,)), ((), ()))
NT = (((1,), (1,)), ((), ()))


def dot(a, b, dims=NN):
    return lax.dot_general(a, b, dims, preferred_element_type=F32)


def kernel(
    sizes,
    x_ref, base_ref, cot_ref, w_ref, bias_ref, routes_ref, gates_ref,
    layer_out, input_grad, base_grad, weight_grad, bias_grad,
    pick, gate_cols, send_c, send_x, xa, xt, ca, wv, part_send, part_recv, own,
    far_send, far_recv, near_send, near_recv, cross_send, cross_back,
    grad_acc, grad_send, grad_back,
    w_sem, c_ss, c_rs, x_ss, x_rs, ag_ss, ag_rs, p_ss, p_rs, far_ss, far_rs,
    near_ss, near_rs, g_ss, g_rs, y_ss, y_rs,
):
    experts, rows, width, lot = sizes
    lot_slots = experts * lot
    slots = CHUNKS * lot_slots
    feats = 2 * width
    half = experts // 2
    middle = half * lot
    me = lax.axis_index("expert")
    tensor = lax.axis_index("tensor")
    chip, core = tensor // 2, lax.rem(tensor, 2)
    other = 1 - core

    def at(step, which):
        return lax.rem(chip + step, 4) * 2 + which

    own_t, left_t, right_t, far_t = at(0, core), at(3, core), at(1, core), at(2, core)
    partner = at(0, other)

    def peer(d):
        return lax.rem(me + d, experts)

    def loop(start, stop, step):
        def run(i, carry):
            step(i)
            return carry

        lax.fori_loop(start, stop, run, 0)

    barrier = pltpu.get_barrier_semaphore()

    def greet(d):
        pl.semaphore_signal(barrier, inc=1, device_id={"expert": peer(d)}, device_id_type=MESH)

    loop(1, experts, greet)
    for t in (partner, left_t, right_t):
        pl.semaphore_signal(barrier, inc=1, device_id={"tensor": t}, device_id_type=MESH)

    def w_copy(t):
        return pltpu.make_async_copy(
            w_ref.at[:, pl.ds(pl.multiple_of(t * width, width), width)], wv.at[t], w_sem.at[t]
        )

    loop(0, 8, lambda t: w_copy(t).start())

    below = (
        lax.broadcasted_iota(jnp.int32, (rows, rows), 1)
        < lax.broadcasted_iota(jnp.int32, (rows, rows), 0)
    ).astype(F32).astype(BF16)
    expert_id = lax.broadcasted_iota(jnp.int32, (rows, experts), 1).astype(F32)
    slot_id = lax.broadcasted_iota(jnp.int32, (rows, slots), 1).astype(F32)
    columns = jnp.concatenate(
        [routes_ref[...].astype(F32), gates_ref[...], jnp.zeros((4, rows), F32)], axis=0
    ).T
    gate_cols[...] = columns
    weighted = (cot_ref[...].astype(F32) * base_ref[...].astype(F32)).astype(BF16).astype(F32)
    sent, before = None, 0.0
    for k in range(2):
        named = (columns[:, k : k + 1] == expert_id).astype(F32)
        place = jnp.sum(
            named * (before + dot(below, named.astype(BF16))), axis=1, keepdims=True
        )
        if k == 0:
            before = jnp.sum(named, axis=0, keepdims=True)
        position = place + float(lot) * jnp.sum(named * expert_id, axis=1, keepdims=True)
        for q in range(1, CHUNKS):
            position += float(lot_slots - lot) * (place >= float(q * lot)).astype(F32)
        chosen = (slot_id == position).astype(F32).astype(BF16)
        pick[k] = chosen
        route_cot = (columns[:, k + 2 : k + 3] * weighted).astype(BF16)
        piece = dot(chosen, route_cot, TN)
        sent = piece if sent is None else sent + piece
    send_c[...] = sent.astype(BF16).reshape(CHUNKS, experts, lot, width)

    def over(src, dst, ss, rs, q, d):
        return pltpu.make_async_remote_copy(
            src_ref=src.at[q, peer(d)], dst_ref=dst.at[q, me], send_sem=ss.at[q, d],
            recv_sem=rs.at[q, me], device_id={"expert": peer(d)}, device_id_type=MESH,
        )

    def exchange(src, dst, ss, rs, q):
        loop(1, experts, lambda d: over(src, dst, ss, rs, q, d).start())

    def landed(dst, ss, rs, q):
        def take(d):
            source = peer(d)
            pltpu.make_async_remote_copy(
                src_ref=dst.at[q, source], dst_ref=dst.at[q, source], send_sem=ss.at[q, d],
                recv_sem=rs.at[q, source], device_id={"expert": source}, device_id_type=MESH,
            ).wait_recv()

        loop(1, experts, take)

    def drain(src, dst, ss, rs):
        for q in range(CHUNKS):
            loop(1, experts, lambda d, q=q: over(src, dst, ss, rs, q, d).wait_send())

    pl.semaphore_wait(barrier, experts + 2)
    ca_own = ca.at[own_t]
    for q in range(CHUNKS):
        exchange(send_c, ca_own, c_ss, c_rs, q)
    both = pick[0] + pick[1]
    for p in range(2):
        sent = dot(both, x_ref[:, p, :], TN).astype(BF16)
        send_x[:, :, :, p * width : (p + 1) * width] = sent.reshape(CHUNKS, experts, lot, width)
    for q in range(CHUNKS):
        exchange(send_x, xa, x_ss, x_rs, q)
        ca[own_t, q, me] = send_c[q, me]
        xa[q, me] = send_x[q, me]

    low, high, whole = pl.ds(0, half), pl.ds(half, half), pl.ds(0, experts)
    moves = [
        (own_t, low, right_t, left_t),
        (own_t, high, right_t, left_t),
        (own_t, high, left_t, right_t),
        (own_t, low, left_t, right_t),
        (own_t, whole, partner, partner),
        (left_t, low, right_t, far_t),
        (right_t, high, left_t, far_t),
        (left_t, whole, partner, at(3, other)),
        (right_t, whole, partner, at(1, other)),
        (far_t, whole, partner, at(2, other)),
    ]

    def move(i, q):
        block, part, target, _ = moves[i]
        region = ca.at[block, q, part]
        return pltpu.make_async_remote_copy(
            src_ref=region, dst_ref=region, send_sem=ag_ss.at[i, q], recv_sem=ag_rs.at[i, q],
            device_id={"tensor": target}, device_id_type=MESH,
        )

    def arrived(i, q):
        _, part, _, block = moves[i]
        region = ca.at[block, q, part]
        pltpu.make_async_remote_copy(
            src_ref=region, dst_ref=region, send_sem=ag_ss.at[i, q], recv_sem=ag_rs.at[i, q],
            device_id={"tensor": partner}, device_id_type=MESH,
        ).wait_recv()

    def arrived_all(i):
        for q in range(CHUNKS):
            arrived(i, q)

    for q in range(CHUNKS):
        landed(ca_own, c_ss, c_rs, q)
        for i in (0, 2, 1, 3, 4):
            move(i, q).start()

    def cot_block(t):
        return ca[t].reshape(slots, width)

    def grads_of(t):
        return dot(cot_block(t), wv[t], NT)

    def add_grads(t):
        grad_acc[...] += grads_of(t)

    def pass_on(q):
        arrived(0, q)
        move(5, q).start()
        arrived(2, q)
        move(6, q).start()
        arrived(1, q)
        move(7, q).start()
        arrived(3, q)
        move(8, q).start()

    def partial(t, q):
        return dot(xa[q].reshape(lot_slots, feats), wv[t])

    def pair(k, q):
        return pltpu.make_async_remote_copy(
            src_ref=part_send.at[k, q], dst_ref=part_recv.at[k, q], send_sem=p_ss.at[k, q],
            recv_sem=p_rs.at[k, q], device_id={"tensor": partner}, device_id_type=MESH,
        )

    def ring(send, recv, ss, rs, i, q):
        return pltpu.make_async_remote_copy(
            src_ref=send.at[i, q], dst_ref=recv.at[i, q], send_sem=ss.at[i, q],
            recv_sem=rs.at[i, q], device_id={"tensor": (right_t, left_t)[i]},
            device_id_type=MESH,
        )

    def far(i, q):
        return ring(far_send, far_recv, far_ss, far_rs, i, q)

    def near(i, q):
        return ring(near_send, near_recv, near_ss, near_rs, i, q)

    def to_partner(k, q):
        part_send[k, q] = partial(at(k, other), q).astype(BF16)
        pair(k, q).start()

    def to_far(q):
        mine = partial(far_t, q)
        pair(2, q).wait_recv()
        total = (mine + part_recv[2, q].astype(F32)).astype(BF16)
        far_send[0, q] = total[:middle]
        far_send[1, q] = total[middle:]
        far(0, q).start()
        far(1, q).start()

    def chip_sum(i, k, q):
        mine = partial(at(k, core), q)
        pair(k, q).wait_recv()
        own[i, q] = mine + part_recv[k, q].astype(F32)

    def to_near(q):
        for i in range(2):
            far(i, q).wait_recv()
            rest, keep = pl.ds(i * middle, middle), pl.ds((1 - i) * middle, middle)
            near_send[i, q, rest] = (own[i, q, rest] + far_recv[i, q].astype(F32)).astype(BF16)
            near_send[i, q, keep] = own[i, q, keep].astype(BF16)
            near(i, q).start()

    def to_rows(q):
        near(0, q).wait_recv()
        near(1, q).wait_recv()
        cross = own[2, q] + near_recv[0, q].astype(F32) + near_recv[1, q].astype(F32)
        cross = (cross + bias_ref[...]).astype(BF16)
        cross_send[q] = cross.reshape(experts, lot, width)
        exchange(cross_send, cross_back, y_ss, y_rs, q)
        cross_back[q, me] = cross_send[q, me]

    scale = 1.0 / (2.0 * rows) ** 0.5
    bias_grad[...] = jnp.sum(cot_block(own_t).astype(F32), axis=0, keepdims=True) * scale
    loop(0, 8, lambda t: w_copy(t).wait())
    grad_acc[...] = grads_of(own_t)
    pass_on(0)
    arrived_all(4)
    add_grads(partner)
    pass_on(1)
    landed(xa, x_ss, x_rs, 0)
    to_partner(2, 0)
    pass_on(2)
    landed(xa, x_ss, x_rs, 1)
    to_partner(2, 1)
    to_far(0)
    add_grads(left_t)
    add_grads(right_t)
    landed(xa, x_ss, x_rs, 2)
    to_partner(2, 2)
    to_far(1)
    to_far(2)
    arrived_all(7)
    add_grads(at(3, other))
    arrived_all(8)
    add_grads(at(1, other))
    for q in range(CHUNKS):
        arrived(5, q)
        arrived(6, q)
        move(9, q).start()
    add_grads(far_t)
    loop(0, 2 * CHUNKS, lambda n: to_partner(1 + 2 * lax.rem(n, 2), n // 2))
    arrived_all(9)
    grad_send[...] = (
        (grad_acc[...] + grads_of(at(2, other)))
        .astype(BF16)
        .reshape(CHUNKS, experts, lot, feats)
    )
    for q in range(CHUNKS):
        exchange(grad_send, grad_back, g_ss, g_rs, q)
        grad_back[q, me] = grad_send[q, me]
    loop(0, 2 * CHUNKS, lambda n: chip_sum(lax.rem(n, 2), 1 + 2 * lax.rem(n, 2), n // 2))
    loop(0, CHUNKS, to_near)
    loop(0, CHUNKS, lambda q: to_partner(0, q))
    loop(0, CHUNKS, lambda q: chip_sum(2, 0, q))

    xt[...] = xa[...].reshape(slots, feats).T

    def weight_block(t):
        columns = pl.ds(pl.multiple_of(t * width, width), width)
        weight_grad[:, columns] = (dot(xt[...], cot_block(t)) * scale).astype(BF16)

    loop(0, 4, weight_block)
    to_rows(0)
    loop(4, 6, weight_block)
    to_rows(1)
    loop(6, 8, weight_block)
    to_rows(2)

    gate0, gate1 = gate_cols[:, 2:3], gate_cols[:, 3:4]
    gate_total = gate0 + gate1
    cot = cot_ref[...].astype(F32)
    for q in range(CHUNKS):
        landed(grad_back, g_ss, g_rs, q)
    grad_sum = dot(pick[0] + pick[1], grad_back[...].reshape(slots, feats))
    input_grad[:, 0, :] = (grad_sum[:, :width] + gate_total * cot).astype(BF16)
    input_grad[:, 1, :] = grad_sum[:, width:].astype(BF16)

    for q in range(CHUNKS):
        landed(cross_back, y_ss, y_rs, q)
    back = cross_back[...].reshape(slots, width)
    mixture = gate0 * dot(pick[0], back) + gate1 * dot(pick[1], back)
    layer_out[...] = (
        base_ref[...].astype(F32) * mixture + gate_total * x_ref[:, 0, :].astype(F32)
    ).astype(BF16)
    base_grad[...] = (cot * mixture).astype(BF16)

    drain(send_c, ca_own, c_ss, c_rs)
    drain(send_x, xa, x_ss, x_rs)
    for q in range(CHUNKS):
        for i in range(10):
            move(i, q).wait_send()
        for k in range(4):
            pair(k, q).wait_send()
        for i in range(2):
            far(i, q).wait_send()
            near(i, q).wait_send()
    drain(grad_send, grad_back, g_ss, g_rs)
    drain(cross_send, cross_back, y_ss, y_rs)


def store(*refs):
    copies = [pltpu.make_async_copy(refs[i], refs[5 + i], refs[10].at[i]) for i in range(5)]
    for copy in copies:
        copy.start()
    for copy in copies:
        copy.wait()


def per_device(layer_input, base_input, cotangent, cross_weight, cross_bias, routes, gate_values):
    rows, _, width = layer_input.shape
    full_out = cross_weight.shape[3]
    experts = lax.axis_size("expert")
    cap = (3 * rows + experts - 1) // experts
    lot = cap // CHUNKS
    slots, feats = experts * cap, 2 * width
    vmem = pl.BlockSpec(memory_space=pltpu.VMEM)
    hbm = pl.BlockSpec(memory_space=pl.ANY)
    dma = pltpu.SemaphoreType.DMA

    def routed(features):
        return [pltpu.VMEM((CHUNKS, experts, lot, features), BF16)]

    def pairs(*shape):
        return [dma(shape), dma(shape)]

    results = pl.pallas_call(
        functools.partial(kernel, (experts, rows, width, lot)),
        out_shape=(
            pltpu.VMEM((rows, width), BF16),
            pltpu.VMEM((rows, 2, width), BF16),
            pltpu.VMEM((rows, width), BF16),
            pltpu.VMEM((feats, full_out), BF16),
            pltpu.VMEM((1, width), F32),
        ),
        in_specs=[vmem, vmem, vmem, hbm, vmem, vmem, vmem],
        out_specs=(vmem, vmem, vmem, vmem, vmem),
        scratch_shapes=[
            pltpu.VMEM((2, rows, slots), BF16),
            pltpu.VMEM((rows, 8), F32),
            *routed(width), *routed(feats), *routed(feats),
            pltpu.VMEM((feats, slots), BF16),
            pltpu.VMEM((8, CHUNKS, experts, lot, width), BF16),
            pltpu.VMEM((8, feats, width), BF16),
            pltpu.VMEM((4, CHUNKS, experts * lot, width), BF16),
            pltpu.VMEM((4, CHUNKS, experts * lot, width), BF16),
            pltpu.VMEM((3, CHUNKS, experts * lot, width), F32),
            pltpu.VMEM((2, CHUNKS, experts // 2 * lot, width), BF16),
            pltpu.VMEM((2, CHUNKS, experts // 2 * lot, width), BF16),
            pltpu.VMEM((2, CHUNKS, experts * lot, width), BF16),
            pltpu.VMEM((2, CHUNKS, experts * lot, width), BF16),
            *routed(width), *routed(width),
            pltpu.VMEM((slots, feats), F32),
            *routed(feats), *routed(feats),
            dma((8,)),
            *pairs(CHUNKS, experts), *pairs(CHUNKS, experts),
            *pairs(10, CHUNKS), *pairs(4, CHUNKS), *pairs(2, CHUNKS), *pairs(2, CHUNKS),
            *pairs(CHUNKS, experts), *pairs(CHUNKS, experts),
        ],
        compiler_params=pltpu.CompilerParams(
            collective_id=0, has_side_effects=True, vmem_limit_bytes=52 * 1024 * 1024
        ),
        name="cross_experts",
    )(
        layer_input, base_input, cotangent,
        cross_weight.reshape(feats, full_out), cross_bias, routes.T, gate_values.T,
    )
    layer_out, input_grad, base_grad, weight_grad, bias_grad = pl.pallas_call(
        store,
        out_shape=tuple(jax.ShapeDtypeStruct(r.shape, r.dtype) for r in results),
        in_specs=[hbm] * 5,
        out_specs=(hbm,) * 5,
        scratch_shapes=[dma((5,))],
        compiler_params=pltpu.CompilerParams(vmem_limit_bytes=1024 * 1024),
        name="store",
    )(*results)
    return (
        layer_out,
        input_grad,
        base_grad,
        weight_grad.reshape(1, 2, width, full_out),
        bias_grad,
    )


def solution(mesh):
    in_specs = (
        P("expert", None, "tensor"),
        P("expert", "tensor"),
        P("expert", "tensor"),
        P("expert", None, "tensor", None),
        P("expert", "tensor"),
        P("expert", None),
        P("expert", None),
    )
    out_specs = (
        P("expert", "tensor"),
        P("expert", None, "tensor"),
        P("expert", "tensor"),
        P("expert", None, "tensor", None),
        P("expert", "tensor"),
    )
    return jax.shard_map(
        per_device, mesh=mesh, in_specs=in_specs, out_specs=out_specs, check_vma=False
    )
```
